32 devices in a mesh: gx: 8 (over z, core), gy: 4 (over y, x).
Axes of the slice: x: 2, y: 2, z: 4, core: 2. Of those that a mesh axis runs over, the one named last changes fastest.
Arguments:
- init_re: float32 [1, 256, 4096], P(None, 'gx', 'gy'), may hold values from -6 to 6
- init_im: float32 [1, 256, 4096], P(None, 'gx', 'gy'), may hold values from -6 to 6
- onsite: float32 [256, 4096], P('gx', 'gy'), may hold values from -0.9 to 0.9
- bond_x: int32 [256, 4096], P('gx', 'gy'), may hold values from 0 to 15
- bond_y: int32 [256, 4096], P('gx', 'gy'), may hold values from 0 to 15
- hop_table: float32 [16], replicated, may hold values from 1.4 to 1.6
- centre: int32 [1, 2], replicated, may hold values from 0 to 255
- duration: float32 [1], replicated, may hold values from 0.55 to 0.6
Outputs:
- out_re: float32 [1, 256, 4096], P(None, 'gx', 'gy')
- out_im: float32 [1, 256, 4096], P(None, 'gx', 'gy')
- term_norms: float32 [2, 8, 1], replicated
The draws below stay inside these ranges and needn't reach their ends.
All inputs are finite; a program needn't handle non-finite values.
Results may differ from the reference program's by a relative error of at most 0.0003.
Values sent between devices are 32-bit elements; how exact they have to be, the bound alone decides.
A program may use at most 64 MiB of HBM per device.

```python
import math
import jax
import jax.numpy as jnp
from jax import lax

PACKETS = 1
TERMS = 8
STEPS = 2
CLASSES = 16
NX = 256
NY = 4096


def draw_onsite(key, part):
    sign_key = jax.random.fold_in(key, 101)
    size_key = jax.random.fold_in(key, 102)
    coin = jax.random.uniform(sign_key, (NX, NY), jnp.float32)
    signs = jnp.where(coin < 0.5, -1.0, 1.0).astype(jnp.float32)
    magnitude = jax.random.uniform(size_key, (NX, NY), jnp.float32, 0.5, 0.9)
    return (signs * magnitude).astype(jnp.float32)


def draw_hop_table(key, part):
    table_key = jax.random.fold_in(key, 201)
    values = jax.random.uniform(table_key, (CLASSES,), jnp.float32, 1.4, 1.6)
    return values.astype(jnp.float32)


def draw_duration(key, part):
    time_key = jax.random.fold_in(key, 301)
    values = jax.random.uniform(time_key, (1,), jnp.float32, 0.55, 0.6)
    return values.astype(jnp.float32)


def place_ends(drawn, own_key, low, largest):
    longest = drawn.shape.index(max(drawn.shape))
    spots = []
    for shift in (0, 1):
        where = [jax.random.randint(jax.random.fold_in(own_key, axis), (), 0, length) for axis, length in enumerate(drawn.shape)]
        where[longest] = (where[longest] + shift) % drawn.shape[longest]
        spots.append(tuple(where))
    return drawn.at[spots[0]].set(low).at[spots[1]].set(largest)


def steps_of(own_key, dims, cuts, least, top_value):
    factor_of, own = 1.0, jax.random.fold_in(own_key, 6)
    for position, blocks in cuts:
        heights = jnp.exp(jax.random.uniform(jax.random.fold_in(own, position), (blocks,), jnp.float32, least / len(cuts), top_value / len(cuts)))
        factor_of = factor_of * jnp.repeat(heights, dims[position] // blocks).reshape([-1 if axis == position else 1 for axis in range(len(dims))])
    return factor_of


def noise(stream_key, dims, spread, bound, split=(), held_as=jnp.bfloat16):
    loudness = steps_of(stream_key, dims, split, -0.22, 0.18) if split else 1.0
    entries = jax.random.normal(stream_key, dims, jnp.float32) * spread * loudness
    return jnp.minimum(jnp.maximum(entries, -bound), bound).astype(held_as)


def setup_inputs(seed: int = 0) -> dict:
    key_list = jax.random.split(jax.random.key(seed), 9)
    init_re = noise(key_list[0], (PACKETS, NX, NY), 1.0, 6.0, ((1, 8), (2, 4)), jnp.float32)
    init_im = noise(key_list[1], (PACKETS, NX, NY), 1.0, 6.0, ((1, 8), (2, 4)), jnp.float32)
    onsite = draw_onsite(jax.random.fold_in(key_list[8], 71), 0)
    bond_x = place_ends(jax.random.randint(key_list[3], (NX, NY), 0, CLASSES), jax.random.fold_in(key_list[3], 1), 0, CLASSES - 1).astype(jnp.int32)
    bond_y = place_ends(jax.random.randint(key_list[4], (NX, NY), 0, CLASSES), jax.random.fold_in(key_list[4], 1), 0, CLASSES - 1).astype(jnp.int32)
    hop_table = draw_hop_table(jax.random.fold_in(key_list[8], 71), 0)
    centre = jax.random.randint(key_list[6], (PACKETS, 2), 0, min(NX, NY)).astype(jnp.int32)
    duration = draw_duration(jax.random.fold_in(key_list[8], 71), 0)
    return dict(init_re=init_re, init_im=init_im, onsite=onsite, bond_x=bond_x, bond_y=bond_y, hop_table=hop_table, centre=centre, duration=duration)


SPECTRAL = 7.5
epsilon = 1e-06

def bessel_weights(duration):
    argument = duration[0] * SPECTRAL
    halved = argument * 0.5
    weights = []
    for degree in range(TERMS):
        series = halved ** degree / math.factorial(degree)
        summed = series
        for counter in range(1, 24):
            series = series * -(halved * halved) / (counter * (counter + degree))
            summed = summed + series
        weights.append(summed if degree == 0 else 2.0 * summed)
    return weights

def rotated(degree, real_part, imag_part):
    quarter = degree % 4
    if quarter == 0:
        return (real_part, imag_part)
    if quarter == 1:
        return (imag_part, -real_part)
    if quarter == 2:
        return (-real_part, -imag_part)
    return (-imag_part, real_part)

def falloff(positions, centres, extent):
    distance = jnp.mod(positions - centres, extent)
    distance = jnp.minimum(distance, extent - distance).astype(jnp.float32)
    return distance * distance * (4.5 / (extent * extent))

def hamiltonian(grid_field, onsite, hop_down, hop_up, hop_right, hop_left):
    result = onsite * grid_field
    result = result - hop_down * jnp.roll(grid_field, -1, 1)
    result = result - hop_up * jnp.roll(grid_field, 1, 1)
    result = result - hop_right * jnp.roll(grid_field, -1, 2)
    result = result - hop_left * jnp.roll(grid_field, 1, 2)
    return result * (1.0 / SPECTRAL)

def reference(init_re, init_im, onsite, bond_x, bond_y, hop_table, centre, duration):
    hop_down = hop_table[bond_x]
    hop_right = hop_table[bond_y]
    hop_up = jnp.roll(hop_down, 1, 0)
    hop_left = jnp.roll(hop_right, 1, 1)
    weights = bessel_weights(duration)
    cell_count = NX * NY
    row_ids = jnp.arange(NX, dtype=jnp.int32)
    col_ids = jnp.arange(NY, dtype=jnp.int32)

    def one_packet(inputs):
        real_init, imag_init, centres = inputs
        row_fall = falloff(row_ids, centres[0], NX)
        col_fall = falloff(col_ids, centres[1], NY)
        envelope = jnp.exp(-(row_fall[:, None] + col_fall[None, :]))
        packet_state = jnp.stack([real_init * envelope, imag_init * envelope])
        norm_rows = []
        for repeat in range(STEPS):
            previous = packet_state
            current = packet_state
            accumulate = weights[0] * packet_state
            norm_list = [jnp.sum(packet_state * packet_state) / cell_count]
            for degree in range(1, TERMS):
                applied = hamiltonian(current, onsite, hop_down, hop_up, hop_right, hop_left)
                following = applied if degree == 1 else 2.0 * applied - previous
                previous, current = (current, following)
                real_rot, imag_rot = rotated(degree, following[0], following[1])
                accumulate = accumulate + weights[degree] * jnp.stack([real_rot, imag_rot])
                norm_list.append(jnp.sum(following * following) / cell_count)
            rescale = lax.rsqrt(jnp.sum(accumulate * accumulate) / cell_count + epsilon)
            packet_state = accumulate * rescale
            norm_rows.append(jnp.stack(norm_list))
        return (packet_state[0], packet_state[1], jnp.stack(norm_rows))
    real_out, imag_out, norm_table = lax.map(one_packet, (init_re, init_im, centre))
    return (real_out, imag_out, jnp.transpose(norm_table, (1, 2, 0)))
```

```python
import functools
import math

import jax
import jax.numpy as jnp
from jax import lax
from jax.experimental import pallas as pl
from jax.experimental.pallas import tpu as pltpu
from jax.sharding import PartitionSpec as P

TERMS = 8
STEPS = 2
SPECTRAL = 7.5
EPSILON = 1e-06
REACH = TERMS - 1
DEPTH = STEPS * REACH
SUB = 8
LANES = 128
SLOT = 16
HALO = -(-DEPTH // SUB) * SUB
PAD = SUB
MESH = pl.DeviceIdType.MESH


def signed(degree):
    return (((0, 1), (1, 1)), ((1, 1), (0, -1)), ((0, -1), (1, -1)), ((1, -1), (0, 1)))[degree % 4]


def bessel_weights(duration):
    halved = duration * (SPECTRAL * 0.5)
    square = halved * halved
    weights = []
    power = jnp.ones_like(halved)
    for degree in range(TERMS):
        series = power * (1.0 / math.factorial(degree))
        summed = series
        for counter in range(1, 24):
            series = series * (square * (-1.0 / (counter * (counter + degree))))
            summed = summed + series
        weights.append(summed if degree == 0 else 2.0 * summed)
        power = power * halved
    return weights


def falloff(position, centre, extent):
    position = jnp.where(position < 0, position + extent, position)
    position = jnp.where(position >= extent, position - extent, position)
    distance = position - centre
    distance = jnp.where(distance < 0, distance + extent, distance)
    distance = jnp.minimum(distance, extent - distance).astype(jnp.float32)
    return jnp.exp(-(distance * distance * (4.5 / (extent * extent))))


def kernel(
    gx, gy, table_ref, centre_ref, duration_ref, re_hbm, im_hbm, on_hbm, bx_hbm, by_hbm,
    out_re, out_im, scale_ref, norms_ref,
    in_re, in_im, in_on, in_bx, in_by, main, odd, first, pack, edge, message, slots,
    load_sem, send_sem, recv_sem, sum_send, sum_recv,
):
    rows, cols = in_on.shape
    tiles = cols // LANES
    extended = rows + 2 * HALO
    me_x, me_y = lax.axis_index("gx"), lax.axis_index("gy")
    devices = gx * gy
    me = me_x * gy + me_y

    barrier = pltpu.get_barrier_semaphore()

    def peer(step):
        other = lax.rem(me + step, devices)
        return (other // gy, lax.rem(other, gy))

    def greet(step, carry):
        pl.semaphore_signal(barrier, inc=1, device_id=peer(step), device_id_type=MESH)
        return carry

    loads = [
        pltpu.make_async_copy(source, target, load_sem.at[index])
        for index, (source, target) in enumerate(
            ((by_hbm, in_by), (bx_hbm, in_bx), (on_hbm, in_on), (re_hbm.at[0], in_re), (im_hbm.at[0], in_im))
        )
    ]
    for load in loads:
        load.start()
    lax.fori_loop(1, devices, greet, 0)

    lane = lax.broadcasted_iota(jnp.int32, (SUB, LANES), 1)
    sublane = lax.broadcasted_iota(jnp.int32, (SUB, LANES), 0)
    table = jnp.zeros((SUB, LANES), jnp.float32)
    for index in range(table_ref.shape[0]):
        table = jnp.where(lane == index, table_ref[index], table)
    table = table * (2.0 / SPECTRAL)
    weights = bessel_weights(jnp.full((SUB, LANES), duration_ref[0], jnp.float32))
    row_env = [
        falloff(me_x * rows + tile * SUB + sublane, centre_ref[0, 0], gx * rows)
        for tile in range(rows // SUB)
    ]
    col_env = [
        falloff(me_y * cols + tile * LANES + lane, centre_ref[0, 1], gy * cols)
        for tile in range(tiles)
    ]
    for load in loads:
        load.wait()

    def lookup(index):
        return jnp.take_along_axis(table, index, axis=1, mode="promise_in_bounds")

    own = PAD + HALO
    start_norm = jnp.zeros((SUB, LANES), jnp.float32)
    for r in range(rows // SUB):
        span = slice(r * SUB, r * SUB + SUB)
        held = slice(own + r * SUB, own + r * SUB + SUB)
        for t in (0, tiles - 1, *range(1, tiles - 1)):
            across = slice(t * LANES, t * LANES + LANES)
            envelope = row_env[r] * col_env[t]
            values = (
                in_re[span, across] * envelope,
                in_im[span, across] * envelope,
                in_on[span, across] * (2.0 / SPECTRAL),
                lookup(in_bx[span, across]),
                lookup(in_by[span, across]),
            )
            start_norm = start_norm + (values[0] * values[0] + values[1] * values[1])
            for a, value in enumerate(values):
                main[a, t, held, :] = value
            if t == 0:
                packed = values[0]
                for a in range(1, 5):
                    moved = pltpu.roll(values[a], SLOT * a, 1)
                    packed = jnp.where(lane >= SLOT * a, moved, packed)
                pack[0, span, :] = packed
            if t == tiles - 1:
                packed = pltpu.roll(values[0], SLOT, 1)
                for a in range(1, 5):
                    moved = pltpu.roll(values[a], SLOT * (a + 1), 1)
                    packed = jnp.where(lane >= SLOT * a, moved, packed)
                pack[1, span, :] = packed

    pl.semaphore_wait(barrier, devices - 1)
    up, down = lax.rem(me_x + gx - 1, gx), lax.rem(me_x + 1, gx)
    west, east = lax.rem(me_y + gy - 1, gy), lax.rem(me_y + 1, gy)
    top, bottom = pl.ds(0, HALO), pl.ds(rows - HALO, HALO)
    copies = []

    def send(source, target, device):
        index = len(copies)
        copy = pltpu.make_async_remote_copy(
            src_ref=source, dst_ref=target, send_sem=send_sem.at[index], recv_sem=recv_sem.at[index],
            device_id=device, device_id_type=MESH,
        )
        copy.start()
        copies.append(copy)

    body = pl.ds(0, tiles)
    for side, aside in ((0, west), (1, east)):
        send(pack.at[side], edge.at[side, pl.ds(HALO, rows)], (me_x, aside))
        send(pack.at[side, top], edge.at[side, pl.ds(HALO + rows, HALO)], (up, aside))
        send(pack.at[side, bottom], edge.at[side, pl.ds(0, HALO)], (down, aside))
    send(
        main.at[:, body, pl.ds(own, HALO)],
        main.at[:, body, pl.ds(own + rows, HALO)],
        (up, me_y),
    )
    send(
        main.at[:, body, pl.ds(own + rows - HALO, HALO)],
        main.at[:, body, pl.ds(PAD, HALO)],
        (down, me_y),
    )
    for copy in copies[:6]:
        copy.wait()
    for r in range(extended // SUB):
        span = slice(r * SUB, r * SUB + SUB)
        held = slice(PAD + r * SUB, PAD + r * SUB + SUB)
        from_east = edge[0, span, :]
        from_west = edge[1, span, :]
        for a in range(5):
            right = pltpu.roll(from_east, (LANES - SLOT * a) % LANES, 1)
            left = pltpu.roll(from_west, (LANES - SLOT * (a + 1)) % LANES, 1)
            main[a, tiles, held, :] = jnp.where(lane < LANES // 2, right, left)
    for copy in copies[6:]:
        copy.wait()

    last_lane = lane == LANES - 1
    first_lane = lane == 0

    def apply(current, target, degree, left_over, total, is_last):
        low = (HALO - left_over) // SUB
        high = -(-(HALO + rows + left_over) // SUB)
        keep = (HALO // SUB, (HALO + rows) // SUB)
        later = left_over if is_last else left_over + degree - REACH
        norm = jnp.zeros((SUB, LANES), jnp.float32)
        for r in range(low, high):
            base = PAD + r * SUB
            here = slice(base, base + SUB)
            above = slice(base - 1, base + SUB - 1)
            below = slice(base + 1, base + SUB + 1)
            owned = keep[0] <= r < keep[1]
            centre = [[current[f, t, here, :] for f in range(2)] for t in range(tiles + 1)]
            cross = [main[4, t, here, :] for t in range(tiles + 1)]
            rights = [[pltpu.roll(centre[t][f], LANES - 1, 1) for f in range(2)] for t in range(tiles + 1)]
            lefts = [[pltpu.roll(cross[t] * centre[t][f], 1, 1) for f in range(2)] for t in range(tiles + 1)]
            for t in range(tiles + 1):
                potential = main[2, t, here, :]
                hop_below = main[3, t, here, :]
                hop_above = main[3, t, above, :]
                fresh = []
                for f in range(2):
                    right = jnp.where(last_lane, rights[(t + 1) % (tiles + 1)][f], rights[t][f])
                    left = jnp.where(first_lane, lefts[t - 1][f], lefts[t][f])
                    value = potential * centre[t][f]
                    value = value - hop_below * current[f, t, below, :]
                    value = value - hop_above * current[f, t, above, :]
                    value = value - cross[t] * right
                    value = value - left
                    if degree == 1:
                        value = value * 0.5
                    else:
                        value = value - target[f, t, here, :]
                    target[f, t, here, :] = value
                    fresh.append(value)
                mine = owned and t < tiles
                if mine:
                    norm = norm + (fresh[0] * fresh[0] + fresh[1] * fresh[1])
                total(r, t, degree, centre[t], fresh, mine)
        return norm

    norms = []
    sums = []

    reach_tiles = ((HALO - REACH) // SUB, -(-(HALO + rows + REACH) // SUB))
    state = {}

    def accumulate(read, write, step):
        def total(r, t, degree, before, fresh, mine):
            if step == STEPS - 1:
                if not mine:
                    return
            elif not reach_tiles[0] <= r < reach_tiles[1]:
                return
            result = []
            for part, (f, sign) in enumerate(signed(degree)):
                base = weights[0] * before[part] if degree == 1 else read(part, r, t)
                term = weights[degree] * fresh[f]
                result.append(base + term if sign > 0 else base - term)
            for part in range(2):
                write(part, r, t, result[part])
            if degree == REACH and mine:
                state["sum"] = state["sum"] + (result[0] * result[0] + result[1] * result[1])
        return total

    def read_first(part, r, t):
        return first[part, t, PAD + r * SUB : PAD + r * SUB + SUB, :]

    def write_first(part, r, t, value):
        first[part, t, PAD + r * SUB : PAD + r * SUB + SUB, :] = value

    outs = (out_re, out_im)

    def place(r, t):
        begin = r * SUB - HALO
        return (0, slice(begin, begin + SUB), slice(t * LANES, t * LANES + LANES))

    def read_out(part, r, t):
        return outs[part][place(r, t)]

    def write_out(part, r, t, value):
        outs[part][place(r, t)] = value

    psi = main
    norms.append(start_norm)
    for step in range(STEPS):
        total = accumulate(*((read_first, write_first) if step == 0 else (read_out, write_out)), step)
        state["sum"] = jnp.zeros((SUB, LANES), jnp.float32)
        if step:
            norms.append(sums[-1])
        buffers = (psi, odd)
        for degree in range(1, TERMS):
            left_over = DEPTH - step * REACH - degree
            norms.append(apply(buffers[(degree + 1) % 2], buffers[degree % 2], degree, left_over, total, step == STEPS - 1))
        sums.append(state["sum"])
        psi = first

    entries = norms + sums
    row = jnp.zeros((1, LANES), jnp.float32)
    for begin in range(0, len(entries), SUB):
        grid = jnp.zeros((SUB, LANES), jnp.float32)
        for offset, entry in enumerate(entries[begin : begin + SUB]):
            grid = jnp.where(sublane == offset, jnp.sum(entry, axis=0, keepdims=True), grid)
        grid = jnp.sum(grid, axis=1, keepdims=True)
        row = row + jnp.sum(jnp.where(lane == sublane + begin, grid, 0.0), axis=0, keepdims=True)
    message[...] = row

    def copy_of(step):
        return pltpu.make_async_remote_copy(
            src_ref=message, dst_ref=slots.at[me], send_sem=sum_send, recv_sem=sum_recv,
            device_id=peer(step), device_id_type=MESH,
        )

    slots[me] = row

    def send_sum(step, carry):
        copy_of(step).start()
        return carry

    lax.fori_loop(1, devices, send_sum, 0)
    others = slots.at[pl.ds(0, devices - 1)]
    pltpu.make_async_copy(others, others, sum_send).wait()
    pltpu.make_async_copy(others, others, sum_recv).wait()
    whole = jnp.sum(slots[...], axis=0) * (1.0 / (devices * rows * cols))
    lane_row = lax.broadcasted_iota(jnp.int32, (1, LANES), 1)
    count = STEPS * TERMS

    def entry_of(index):
        return jnp.sum(jnp.where(lane_row == index, whole, 0.0), axis=1, keepdims=True)

    scale = jnp.ones((1, 1), jnp.float32)
    factor = jnp.ones((1, LANES), jnp.float32)
    for step in range(STEPS):
        factor = jnp.where((lane_row >= step * TERMS) & (lane_row < (step + 1) * TERMS), scale * scale, factor)
        scale = scale * lax.rsqrt(entry_of(count + step) * (scale * scale) + EPSILON)
    norms_ref[...] = whole * factor
    scale_ref[...] = jnp.broadcast_to(scale, (1, LANES))


def per_device(gx, gy, init_re, init_im, onsite, bond_x, bond_y, hop_table, centre, duration):
    packets, rows, cols = init_re.shape
    tiles = cols // LANES
    assert packets == 1 and rows >= HALO
    height = rows + 2 * HALO + 2 * PAD
    f32, i32 = jnp.float32, jnp.int32
    smem = pl.BlockSpec(memory_space=pltpu.SMEM)
    vmem = pl.BlockSpec(memory_space=pltpu.VMEM)
    anywhere = pl.BlockSpec(memory_space=pl.ANY)
    raw_re, raw_im, scale, norms = pl.pallas_call(
        functools.partial(kernel, gx, gy),
        out_shape=(
            jax.ShapeDtypeStruct(init_re.shape, f32),
            jax.ShapeDtypeStruct(init_im.shape, f32),
            jax.ShapeDtypeStruct((1, LANES), f32),
            jax.ShapeDtypeStruct((1, LANES), f32),
        ),
        in_specs=[smem] * 3 + [anywhere] * 5,
        out_specs=[vmem] * 4,
        scratch_shapes=[
            pltpu.VMEM((rows, cols), f32),
            pltpu.VMEM((rows, cols), f32),
            pltpu.VMEM((rows, cols), f32),
            pltpu.VMEM((rows, cols), i32),
            pltpu.VMEM((rows, cols), i32),
            pltpu.VMEM((5, tiles + 1, height, LANES), f32),
            pltpu.VMEM((2, tiles + 1, height, LANES), f32),
            pltpu.VMEM((2, tiles + 1, height, LANES), f32),
            pltpu.VMEM((2, rows, LANES), f32),
            pltpu.VMEM((2, rows + 2 * HALO, LANES), f32),
            pltpu.VMEM((1, LANES), f32),
            pltpu.VMEM((gx * gy, 1, LANES), f32),
            pltpu.SemaphoreType.DMA((5,)),
            pltpu.SemaphoreType.DMA((8,)),
            pltpu.SemaphoreType.DMA((8,)),
            pltpu.SemaphoreType.DMA,
            pltpu.SemaphoreType.DMA,
        ],
        compiler_params=pltpu.CompilerParams(collective_id=0, has_side_effects=True),
        name="chebyshev",
    )(hop_table, centre, duration, init_re, init_im, onsite, bond_x, bond_y)
    factor = scale[0, 0]
    table = norms[0, : STEPS * TERMS].reshape(STEPS, TERMS, 1)
    return raw_re * factor, raw_im * factor, table


def solution(mesh):
    return jax.shard_map(
        functools.partial(per_device, mesh.shape["gx"], mesh.shape["gy"]),
        mesh=mesh,
        in_specs=(
            P(None, "gx", "gy"),
            P(None, "gx", "gy"),
            P("gx", "gy"),
            P("gx", "gy"),
            P("gx", "gy"),
            P(),
            P(),
            P(),
        ),
        out_specs=(P(None, "gx", "gy"), P(None, "gx", "gy"), P()),
        check_vma=False,
    )
```
